32 devices in a mesh: seq: 16 (over z, y, core), exp: 2 (over x).
Axes of the slice: x: 2, y: 2, z: 4, core: 2. Of those that a mesh axis runs over, the one named last changes fastest.
Arguments:
- tokens: bfloat16 [16, 800, 1152], P('seq', 'exp'), may hold values from -6 to 6
- modulation: float32 [16, 2, 1152], P('seq'), may hold values from -1.75 to 1.75
- router: bfloat16 [1152, 4], replicated, may hold values from -0.1875 to 0.1875
- expert_in: bfloat16 [4, 2304, 1152], P('exp', 'seq'), may hold values from -0.1875 to 0.1875
- expert_out: bfloat16 [4, 2304, 1152], P('exp', 'seq'), may hold values from -0.125 to 0.125
- head: bfloat16 [1152, 256], replicated, may hold values from -0.1875 to 0.1875
- expert_ids: int32 [16, 800, 2], P('seq', 'exp'), may hold values from 0 to 3, as said below
- slot_ids: int32 [16, 800, 2], P('seq', 'exp'), may hold values from 0 to 287, as said below
- sensitivity: float32 [16, 8, 2, 320, 320], P('seq', None, None, 'exp'), may hold values from -3 to 3
- kspace: float32 [16, 8, 2, 320, 320], P('seq', None, None, None, 'exp'), may hold values from -6 to 6
- sampled: int32 [16, 320], P('seq'), may hold values 0 or 1
Outputs:
- estimate: float32 [16, 800, 256], P('seq', 'exp')
- guidance: float32 [16, 800, 1152], P('seq', 'exp')
The draws below stay inside these ranges and needn't reach their ends.
Inputs may be any that keep to these rules, and one draw needn't show every extreme that they name: `expert_ids`: the two entries of a row differ. In each aligned block of 400 rows (the rows of one device) no expert is named more than 288 times, and some expert exactly 288 times. `slot_ids`: within each aligned block of 400 rows, the routes that name one expert in expert_ids (same row and column) carry that expert's slots 0, 1, 2 and so on, each once.
All inputs are finite; a program needn't handle non-finite values. No bound on the sum of `sampled` on one device may be relied on, other than what follows from the above.
Results may differ from the reference program's by a relative error of at most 0.0075.
Values may be sent and summed in bfloat16 or wider, within the bound.
A program may use at most 128 MiB of HBM per device.

```python
import jax
import jax.numpy as jnp
from jax import lax

D = 1152
FF = 2304
COILS = 8
H = 320
W = 320
PH = 8
PW = 16
EXPERTS = 4
PV = 256
SLICES = 16
TOK_SLICE = 800
TOK_DEV = 400
CAP = 288


def route_tables(key):
    blocks = SLICES * TOK_SLICE // TOK_DEV
    remaining = 2 * TOK_DEV - CAP

    def one_block(block_key):
        subkeys = jax.random.split(block_key, 5)
        expert_iota = jnp.arange(EXPERTS, dtype=jnp.int32)
        hottest = jax.random.randint(subkeys[0], (), 0, EXPERTS, dtype=jnp.int32)
        weights = jax.random.randint(subkeys[1], (EXPERTS,), 5, 7, dtype=jnp.int32)
        weights = jnp.where(expert_iota == hottest, 0, weights)
        shares = weights * remaining // jnp.sum(weights)
        leftover = remaining - jnp.sum(shares)
        priority = jax.random.permutation(subkeys[2], EXPERTS).astype(jnp.int32)
        priority = jnp.where(expert_iota == hottest, EXPERTS, priority)
        ranking = jnp.sum((priority[None, :] < priority[:, None]).astype(jnp.int32), axis=1)
        counts = shares + (ranking < leftover).astype(jnp.int32)
        counts = jnp.where(expert_iota == hottest, CAP, counts)
        run_ends = jnp.cumsum(counts)
        run_starts = run_ends - counts
        positions = jnp.arange(2 * TOK_DEV, dtype=jnp.int32)
        labels = jnp.sum((run_ends[None, :] <= positions[:, None]).astype(jnp.int32), axis=1)
        label_start = jnp.sum(jnp.where(labels[:, None] == expert_iota[None, :], run_starts[None, :], 0), axis=1)
        places = positions - label_start
        shuffle = jax.random.permutation(subkeys[3], TOK_DEV).astype(jnp.int32)
        first_ids = labels[shuffle]
        second_ids = labels[shuffle + TOK_DEV]
        first_slots = places[shuffle]
        second_slots = places[shuffle + TOK_DEV]
        swapped = jax.random.randint(subkeys[4], (TOK_DEV,), 0, 2, dtype=jnp.int32) == 1
        route_ids = jnp.stack([jnp.where(swapped, second_ids, first_ids), jnp.where(swapped, first_ids, second_ids)], axis=1)
        route_slots = jnp.stack([jnp.where(swapped, second_slots, first_slots), jnp.where(swapped, first_slots, second_slots)], axis=1)
        return (route_ids, route_slots)
    block_keys = jax.random.split(jax.random.fold_in(key, 11), blocks)
    route_ids, route_slots = jax.vmap(one_block)(block_keys)
    return (route_ids.reshape(SLICES, TOK_SLICE, 2).astype(jnp.int32), route_slots.reshape(SLICES, TOK_SLICE, 2).astype(jnp.int32))


def draw_expert_ids(key, part):
    return route_tables(key)[0]


def draw_slot_ids(key, part):
    return route_tables(key)[1]


def plant(array, key, low, largest):
    index_at = [jax.random.randint(jax.random.fold_in(key, axis), (), 0, length) for axis, length in enumerate(array.shape)]
    main_axis = array.shape.index(max(array.shape))
    neighbour = index_at[:main_axis] + [(index_at[main_axis] + 1) % array.shape[main_axis]] + index_at[main_axis + 1:]
    return array.at[tuple(index_at)].set(low).at[tuple(neighbour)].set(largest)


def level_of(own_key, extent, cuts, low, high):
    def one(axis_at, blocks):
        draws = jax.random.uniform(jax.random.fold_in(jax.random.fold_in(own_key, 6), axis_at), (blocks,), jnp.float32, low / len(cuts), high / len(cuts))
        return jnp.repeat(jnp.exp(draws), extent[axis_at] // blocks).reshape((-1,) + (1,) * (len(extent) - axis_at - 1))

    gain = one(*cuts[0])
    for cut in cuts[1:]:
        gain = gain * one(*cut)
    return gain


def noise(own_key, shape, width, reach, cuts=(), kind=jnp.bfloat16):
    array = jax.random.normal(own_key, shape, jnp.float32) * width
    if len(cuts) > 0:
        array = level_of(own_key, shape, cuts, -0.22, 0.18) * array
    return jnp.clip(array, min=-reach, max=reach).astype(kind)


def setup_inputs(seed: int = 0) -> dict:
    splits = jax.random.split(jax.random.key(seed), 12)
    return {
        "tokens": noise(splits[0], (SLICES, TOK_SLICE, D), 1.0, 6.0, ((0, 16), (1, 2))),
        "modulation": noise(splits[1], (SLICES, 2, D), 0.3, 1.75, ((0, 16),), jnp.float32),
        "router": noise(splits[2], (D, EXPERTS), D ** -0.5, 0.1875),
        "expert_in": noise(splits[3], (EXPERTS, FF, D), D ** -0.5, 0.1875, ((0, 2), (1, 16))),
        "expert_out": noise(splits[4], (EXPERTS, FF, D), FF ** -0.5, 0.125, ((0, 2), (1, 16))),
        "head": noise(splits[5], (D, PV), D ** -0.5, 0.1875),
        "expert_ids": draw_expert_ids(jax.random.fold_in(splits[11], 71), 0),
        "slot_ids": draw_slot_ids(jax.random.fold_in(splits[11], 71), 0),
        "sensitivity": noise(splits[8], (SLICES, COILS, 2, H, W), 0.5, 3.0, ((0, 16), (3, 2)), jnp.float32),
        "kspace": noise(splits[9], (SLICES, COILS, 2, H, W), 1.0, 6.0, ((0, 16), (4, 2)), jnp.float32),
        "sampled": plant((jax.random.randint(splits[10], (SLICES, W), 0, 3) < 1).astype(jnp.int32), jax.random.fold_in(splits[10], 1), 0, 1),
    }


norm_epsilon = 1e-06
gelu_factor = 0.7978845608028654
gelu_cubic = 0.044715
highest = lax.Precision.HIGHEST

def gelu_tanh(values):
    bending = jnp.tanh(gelu_factor * (values + gelu_cubic * values * values * values))
    return 0.5 * values * (1.0 + bending)

def gelu_slope(values):
    bending = jnp.tanh(gelu_factor * (values + gelu_cubic * values * values * values))
    return 0.5 * (1.0 + bending) + 0.5 * values * (1.0 - bending * bending) * gelu_factor * (1.0 + 3.0 * gelu_cubic * values * values)

def to_picture(values):
    shaped = values.reshape(SLICES, H // PH, W // PW, 2, PH, PW)
    return shaped.transpose(0, 3, 1, 4, 2, 5).reshape(SLICES, 2, H, W)

def to_patches(picture):
    shaped = picture.reshape(SLICES, 2, H // PH, PH, W // PW, PW)
    return shaped.transpose(0, 2, 4, 1, 3, 5).reshape(SLICES, TOK_SLICE, 2 * PH * PW)

def contract_last(left_side, right_side):
    return lax.dot_general(left_side, right_side, (((1,), (1,)), ((), ())), preferred_element_type=jnp.float32)

def reference(tokens, modulation, router, expert_in, expert_out, head, expert_ids, slot_ids, sensitivity, kspace, sampled):
    token_count = SLICES * TOK_SLICE
    routes = 2 * token_count
    blocks = token_count // TOK_DEV
    tokens_f = tokens.astype(jnp.float32)
    centred = tokens_f - lax.optimization_barrier(jnp.mean(tokens_f, axis=2, keepdims=True))
    inverse = lax.rsqrt(lax.optimization_barrier(jnp.mean(centred * centred, axis=2, keepdims=True)) + norm_epsilon)
    normed = centred * inverse
    scale_rows = modulation[:, 0][:, None, :]
    shift_rows = modulation[:, 1][:, None, :]
    modulated = (normed * (1.0 + scale_rows) + shift_rows).astype(jnp.bfloat16).reshape(token_count, D)
    scale_flat = jnp.broadcast_to(scale_rows, (SLICES, TOK_SLICE, D)).reshape(token_count, D)
    normed = normed.reshape(token_count, D)
    inverse = inverse.reshape(token_count, 1)
    flat_tokens = tokens.reshape(token_count, D)
    route_ids = expert_ids.reshape(token_count, 2).astype(jnp.int32)
    route_slots = slot_ids.reshape(token_count, 2).astype(jnp.int32)
    logits = jnp.dot(modulated, router, preferred_element_type=jnp.float32)
    chosen = jnp.take_along_axis(logits, route_ids, axis=1)
    gate_first = jax.nn.sigmoid(chosen[:, 0] - chosen[:, 1])
    gate_second = 1.0 - gate_first
    block_of = (jnp.arange(token_count, dtype=jnp.int32) // TOK_DEV)[:, None]
    places = ((block_of * EXPERTS + route_ids) * CAP + route_slots).reshape(routes).astype(jnp.int32)
    slot_table = jnp.full((blocks * EXPERTS * CAP,), routes, dtype=jnp.int32)
    slot_table = slot_table.at[places].set(jnp.arange(routes, dtype=jnp.int32))
    slot_table = slot_table.reshape(blocks, EXPERTS, CAP).transpose(1, 0, 2).reshape(EXPERTS, blocks * CAP)
    padded_inputs = jnp.concatenate([modulated, jnp.zeros((1, D), modulated.dtype)], axis=0)

    def token_of(entries):
        return jnp.where(entries < routes, entries // 2, token_count).astype(jnp.int32)

    def forward_expert(running, pieces):
        weight_in, weight_out, entries = pieces
        picked_rows = padded_inputs[token_of(entries)]
        hidden = contract_last(picked_rows, weight_in)
        active = gelu_tanh(hidden).astype(jnp.bfloat16)
        output = jnp.dot(active, weight_out, preferred_element_type=jnp.float32).astype(jnp.bfloat16)
        projected = jnp.dot(output, head, preferred_element_type=jnp.float32).astype(jnp.bfloat16)
        return (running.at[entries].set(projected.astype(jnp.float32)), None)
    projected_routes = lax.scan(forward_expert, jnp.zeros((routes + 1, PV), jnp.float32), (expert_in, expert_out, slot_table))[0]
    proj_pairs = projected_routes[:routes].reshape(token_count, 2, PV)
    estimate = jnp.dot(flat_tokens, head, preferred_element_type=jnp.float32)
    estimate = estimate + gate_first[:, None] * proj_pairs[:, 0] + gate_second[:, None] * proj_pairs[:, 1]
    picture = to_picture(estimate.reshape(SLICES, TOK_SLICE, PV))
    complex_picture = lax.complex(picture[:, 0], picture[:, 1])
    coil_maps = lax.complex(sensitivity[:, :, 0], sensitivity[:, :, 1])
    measured = lax.complex(kspace[:, :, 0], kspace[:, :, 1])
    column_mask = sampled.astype(jnp.float32)[:, None, None, :]
    spectrum = jnp.fft.fft2(coil_maps * complex_picture[:, None], norm='ortho')
    misfit = column_mask * (spectrum - measured)
    pulled = lax.optimization_barrier(jnp.sum(jnp.conj(coil_maps) * jnp.fft.ifft2(misfit, norm='ortho'), axis=1))
    pixel_grad = to_patches(jnp.stack([jnp.real(pulled), jnp.imag(pulled)], axis=1)).reshape(token_count, PV)
    gate_pairs = jnp.stack([gate_first, gate_second], axis=1)
    route_grads = (gate_pairs[:, :, None] * pixel_grad[:, None, :]).astype(jnp.bfloat16).reshape(routes, PV)
    padded_grads = jnp.concatenate([route_grads, jnp.zeros((1, PV), route_grads.dtype)], axis=0)
    gate_grads = lax.optimization_barrier(jnp.sum(pixel_grad[:, None, :] * proj_pairs, axis=2))
    logit_step = (gate_grads[:, 0] - gate_grads[:, 1]) * gate_first * gate_second

    def backward_expert(running, pieces):
        weight_in, weight_out, entries = pieces
        picked_rows = padded_inputs[token_of(entries)]
        hidden = contract_last(picked_rows, weight_in)
        output_grad = contract_last(padded_grads[entries], head).astype(jnp.bfloat16)
        hidden_grad = (contract_last(output_grad, weight_out) * gelu_slope(hidden)).astype(jnp.bfloat16)
        input_grad = jnp.dot(hidden_grad, weight_in, preferred_element_type=jnp.float32).astype(jnp.bfloat16)
        return (running.at[token_of(entries)].add(input_grad.astype(jnp.float32)), None)
    input_grads = lax.scan(backward_expert, jnp.zeros((token_count + 1, D), jnp.float32), (expert_in, expert_out, slot_table))[0][:token_count]
    expert_iota = jnp.arange(EXPERTS, dtype=jnp.int32)[None, :]
    direction = (route_ids[:, 0:1] == expert_iota).astype(jnp.float32) - (route_ids[:, 1:2] == expert_iota).astype(jnp.float32)
    router_grad = lax.dot_general(logit_step[:, None] * direction, router.astype(jnp.float32), (((1,), (1,)), ((), ())), precision=highest)
    modulated_grad = input_grads + router_grad
    scaled = modulated_grad * (1.0 + scale_flat)
    norm_grad = inverse * (scaled - lax.optimization_barrier(jnp.mean(scaled, axis=1, keepdims=True)) - normed * lax.optimization_barrier(jnp.mean(scaled * normed, axis=1, keepdims=True)))
    residual_grad = lax.dot_general(pixel_grad, head.astype(jnp.float32), (((1,), (1,)), ((), ())), precision=highest)
    guidance = residual_grad + norm_grad
    return (estimate.reshape(SLICES, TOK_SLICE, PV), guidance.reshape(SLICES, TOK_SLICE, D))
```

```python
import jax
import jax.numpy as jnp
from jax import lax
from jax.sharding import PartitionSpec as P

PH = 8
PW = 16


norm_epsilon = 1e-06
gelu_factor = 0.7978845608028654
gelu_cubic = 0.044715
highest = lax.Precision.HIGHEST


def from_partner(value, axis, distance):
    mask = 2**distance
    pairs = [(source, source ^ mask) for source in range(lax.axis_size(axis))]
    return lax.ppermute(value, axis, pairs)


def gelu_tanh(values):
    bending = jnp.tanh(gelu_factor * (values + gelu_cubic * values * values * values))
    return 0.5 * values * (1.0 + bending)


def gelu_slope(values):
    bending = jnp.tanh(gelu_factor * (values + gelu_cubic * values * values * values))
    return 0.5 * (1.0 + bending) + 0.5 * values * (1.0 - bending * bending) * gelu_factor * (
        1.0 + 3.0 * gelu_cubic * values * values
    )


def dft_tables(length):
    counter = jnp.arange(length, dtype=jnp.int32)
    product = counter[:, None] * counter[None, :] % length
    angles = product.astype(jnp.float32) * (2.0 * jnp.pi / length)
    factor = 1.0 / jnp.sqrt(jnp.float32(length))
    return (jnp.cos(angles) * factor, jnp.sin(angles) * factor)


def along_width(operand, matrix):
    return jnp.einsum("crw,wk->crk", operand, matrix, preferred_element_type=jnp.float32)


def along_height(matrix, operand):
    return jnp.einsum("kh,chw->ckw", matrix, operand, preferred_element_type=jnp.float32)


def to_experts(buffer):
    arrived = from_partner(buffer[:, 1], "seq", 0)
    rows = [jnp.concatenate([buffer[d, 0], arrived[d]], axis=0) for d in range(buffer.shape[0])]
    return [rows[d] if d == 0 else from_distance(rows[d], d) for d in range(len(rows))]


def to_owners(blocks):
    half = blocks[0].shape[0] // 2
    back = [block if d == 0 else from_distance(block, d) for d, block in enumerate(blocks)]
    partner_rows = from_partner(jnp.stack([block[half:] for block in back]), "seq", 0)
    parts = []
    for d, block in enumerate(back):
        parts += [block[:half], partner_rows[d]]
    return jnp.concatenate(parts, axis=0)


def from_distance(value, distance):
    pairs = [(source, source ^ distance) for source in range(lax.axis_size("exp"))]
    return lax.ppermute(value, "exp", pairs)


def gather_expert(shards, parity):
    own = lax.dynamic_index_in_dim(shards, parity, 0, keepdims=False)
    other = lax.dynamic_index_in_dim(shards, 1 - parity, 0, keepdims=False)
    held = jnp.concatenate([own, from_partner(other, "seq", 0)], axis=0)
    size = lax.axis_size("seq")
    ring = [(source, (source + 4) % size) for source in range(size)]
    parts = []
    for step in range(size // 4):
        parts += [held, from_partner(held, "seq", 1)]
        if step < size // 4 - 1:
            held = lax.ppermute(held, "seq", ring)
    return jnp.concatenate(parts, axis=0)


def contract_last(left_side, right_side):
    return lax.dot_general(
        left_side, right_side, (((1,), (1,)), ((), ())), preferred_element_type=jnp.float32
    )


def on_device(
    tokens,
    modulation,
    router,
    expert_in,
    expert_out,
    head,
    expert_ids,
    slot_ids,
    sensitivity,
    kspace,
    sampled,
):
    tok_rows = tokens.shape[1]
    model_width = tokens.shape[2]
    experts = router.shape[1]
    pixel_values = head.shape[1]
    groups = lax.axis_size("exp")
    seq_size = lax.axis_size("seq")
    capacity = 72 * tok_rows // (25 * experts)
    parity = lax.axis_index("seq") % 2
    group = lax.axis_index("exp")
    weight_in = gather_expert(expert_in, parity)
    weight_out = gather_expert(expert_out, parity)
    flat_tokens = tokens.reshape(tok_rows, model_width)
    route_ids = expert_ids.reshape(tok_rows, 2)
    route_slots = slot_ids.reshape(tok_rows, 2)
    scale_row = modulation[0, 0]
    shift_row = modulation[0, 1]
    tokens_f = flat_tokens.astype(jnp.float32)
    centred = tokens_f - jnp.mean(tokens_f, axis=1, keepdims=True)
    inverse = lax.rsqrt(jnp.mean(centred * centred, axis=1, keepdims=True) + norm_epsilon)
    normed = centred * inverse
    modulated = (normed * (1.0 + scale_row) + shift_row).astype(jnp.bfloat16)
    logits = jnp.dot(modulated, router, preferred_element_type=jnp.float32)
    expert_iota = jnp.arange(experts, dtype=jnp.int32)[None, :]
    first_hot = (route_ids[:, 0:1] == expert_iota).astype(jnp.float32)
    second_hot = (route_ids[:, 1:2] == expert_iota).astype(jnp.float32)
    gate_first = jax.nn.sigmoid(
        jnp.sum(logits * first_hot, axis=1) - jnp.sum(logits * second_hot, axis=1)
    )
    gate_second = 1.0 - gate_first
    near_ids = ((route_ids // 2) ^ group) * 2 + ((route_ids % 2) ^ parity)
    targets = near_ids * capacity + route_slots
    slot_iota = jnp.arange(experts * capacity, dtype=jnp.int32)[:, None]
    first_place = (slot_iota == targets[None, :, 0]).astype(jnp.bfloat16)
    second_place = (slot_iota == targets[None, :, 1]).astype(jnp.bfloat16)
    send_rows = jnp.dot(
        first_place + second_place, modulated, preferred_element_type=jnp.float32
    ).astype(jnp.bfloat16)
    incoming = to_experts(send_rows.reshape(groups, 2, capacity, model_width))
    hidden = [contract_last(rows, weight_in) for rows in incoming]
    projected = [None] * groups
    for d in reversed(range(groups)):
        active = gelu_tanh(hidden[d]).astype(jnp.bfloat16)
        output = jnp.dot(active, weight_out, preferred_element_type=jnp.float32)
        projected[d] = jnp.dot(
            output.astype(jnp.bfloat16), head, preferred_element_type=jnp.float32
        ).astype(jnp.bfloat16)
    gathered = to_owners(projected)
    first_proj = jnp.take(gathered, targets[:, 0], axis=0)
    second_proj = jnp.take(gathered, targets[:, 1], axis=0)
    estimate = jnp.dot(flat_tokens, head, preferred_element_type=jnp.float32)
    estimate = (
        estimate
        + gate_first[:, None] * first_proj.astype(jnp.float32)
        + gate_second[:, None] * second_proj.astype(jnp.float32)
    )
    full_width = sensitivity.shape[4]
    rows_here = sensitivity.shape[3]
    patch_rows = rows_here // PH
    patch_cols = full_width // PW
    picture = (
        estimate.reshape(patch_rows, patch_cols, 2, PH, PW)
        .transpose(2, 0, 3, 1, 4)
        .reshape(2, rows_here, full_width)
    )
    sens_real = sensitivity[0, :, 0]
    sens_imag = sensitivity[0, :, 1]
    coil_real = sens_real * picture[0] - sens_imag * picture[1]
    coil_imag = sens_real * picture[1] + sens_imag * picture[0]
    cos_width, sin_width = dft_tables(full_width)
    full_height = kspace.shape[3]
    block_cols = kspace.shape[4]
    cos_height, sin_height = dft_tables(full_height)
    short = jnp.bfloat16

    def rows_of(table, block):
        return lax.dynamic_slice_in_dim(table, (group ^ block) * block_cols, block_cols, 0)

    def height_rows_of(table, block):
        return lax.dynamic_slice_in_dim(table, (group ^ block) * rows_here, rows_here, 0)

    cos_w = [rows_of(cos_width, d).astype(short) for d in range(groups)]
    sin_w = [rows_of(sin_width, d).astype(short) for d in range(groups)]
    cos_h = [height_rows_of(cos_height, d).astype(short) for d in range(groups)]
    sin_h = [height_rows_of(sin_height, d).astype(short) for d in range(groups)]
    coil_real = coil_real.astype(short)
    coil_imag = coil_imag.astype(short)
    mask_full = sampled[0].astype(jnp.float32)
    mask_block = lax.dynamic_slice_in_dim(mask_full, group * block_cols, block_cols)
    measured_real = kspace[0, :, 0]
    measured_imag = kspace[0, :, 1]
    columns = [None] * groups
    for d in reversed(range(groups)):
        row_real = along_width(coil_real, cos_w[d].T) + along_width(coil_imag, sin_w[d].T)
        row_imag = along_width(coil_imag, cos_w[d].T) - along_width(coil_real, sin_w[d].T)
        pair = (row_real.astype(short), row_imag.astype(short))
        columns[d] = pair if d == 0 else tuple(from_distance(part, d) for part in pair)
    spectrum_real = 0.0
    spectrum_imag = 0.0
    for d in range(groups):
        column_real, column_imag = columns[d]
        spectrum_real += along_height(cos_h[d].T, column_real) + along_height(
            sin_h[d].T, column_imag
        )
        spectrum_imag += along_height(cos_h[d].T, column_imag) - along_height(
            sin_h[d].T, column_real
        )
    misfit_real = (mask_block * (spectrum_real - measured_real)).astype(short)
    misfit_imag = (mask_block * (spectrum_imag - measured_imag)).astype(short)
    hybrid = [None] * groups
    for d in reversed(range(groups)):
        pulled_real = along_height(cos_h[d], misfit_real) - along_height(sin_h[d], misfit_imag)
        pulled_imag = along_height(cos_h[d], misfit_imag) + along_height(sin_h[d], misfit_real)
        pair = (pulled_real.astype(short), pulled_imag.astype(short))
        hybrid[d] = pair if d == 0 else tuple(from_distance(part, d) for part in pair)
    adjoint_real = 0.0
    adjoint_imag = 0.0
    for d in range(groups):
        hybrid_real, hybrid_imag = hybrid[d]
        adjoint_real += along_width(hybrid_real, cos_w[d]) - along_width(hybrid_imag, sin_w[d])
        adjoint_imag += along_width(hybrid_imag, cos_w[d]) + along_width(hybrid_real, sin_w[d])
    sum_real = jnp.sum(sens_real * adjoint_real + sens_imag * adjoint_imag, axis=0)
    sum_imag = jnp.sum(sens_real * adjoint_imag - sens_imag * adjoint_real, axis=0)
    pixel_grad = (
        jnp.stack([sum_real, sum_imag])
        .reshape(2, patch_rows, PH, patch_cols, PW)
        .transpose(1, 3, 0, 2, 4)
        .reshape(tok_rows, pixel_values)
    )
    first_grad = (gate_first[:, None] * pixel_grad).astype(jnp.bfloat16)
    second_grad = (gate_second[:, None] * pixel_grad).astype(jnp.bfloat16)
    gate_first_grad = jnp.sum(pixel_grad * first_proj.astype(jnp.float32), axis=1)
    gate_second_grad = jnp.sum(pixel_grad * second_proj.astype(jnp.float32), axis=1)
    logit_step = (gate_first_grad - gate_second_grad) * gate_first * gate_second
    send_back = jnp.dot(first_place, first_grad, preferred_element_type=jnp.float32) + jnp.dot(
        second_place, second_grad, preferred_element_type=jnp.float32
    )
    arriving = to_experts(
        send_back.astype(jnp.bfloat16).reshape(groups, 2, capacity, pixel_values)
    )
    input_grad = [None] * groups
    for d in reversed(range(groups)):
        output_grad = contract_last(arriving[d], head).astype(jnp.bfloat16)
        hidden_grad = (contract_last(output_grad, weight_out) * gelu_slope(hidden[d])).astype(
            jnp.bfloat16
        )
        input_grad[d] = jnp.dot(
            hidden_grad, weight_in, preferred_element_type=jnp.float32
        ).astype(jnp.bfloat16)
    returned = to_owners(input_grad)
    first_input = jnp.take(returned, targets[:, 0], axis=0).astype(jnp.float32)
    second_input = jnp.take(returned, targets[:, 1], axis=0).astype(jnp.float32)
    logit_grad = logit_step[:, None] * (first_hot - second_hot)
    router_grad = lax.dot_general(
        logit_grad, router.astype(jnp.float32), (((1,), (1,)), ((), ())), precision=highest
    )
    modulated_grad = first_input + second_input + router_grad
    scaled = modulated_grad * (1.0 + scale_row)
    norm_grad = inverse * (
        scaled
        - jnp.mean(scaled, axis=1, keepdims=True)
        - normed * jnp.mean(scaled * normed, axis=1, keepdims=True)
    )
    residual_grad = lax.dot_general(
        pixel_grad, head.astype(jnp.float32), (((1,), (1,)), ((), ())), precision=highest
    )
    guidance = residual_grad + norm_grad
    return (estimate.reshape(1, tok_rows, pixel_values), guidance.reshape(1, tok_rows, model_width))


def solution(mesh):
    placed = (
        P("seq", "exp", None),
        P("seq", None, None),
        P(),
        P("exp", "seq", None),
        P("exp", "seq", None),
        P(),
        P("seq", "exp", None),
        P("seq", "exp", None),
        P("seq", None, None, "exp", None),
        P("seq", None, None, None, "exp"),
        P("seq", None),
    )
    return jax.shard_map(
        on_device,
        mesh=mesh,
        in_specs=placed,
        out_specs=(P("seq", "exp", None), P("seq", "exp", None)),
        check_vma=False,
    )
```
